32 devices in a mesh: pipe: 4 (over z), expert: 4 (over y, core), dp: 2 (over x).
Axes of the slice: x: 2, y: 2, z: 4, core: 2. Of those that a mesh axis runs over, the one named last changes fastest.
Arguments:
- tokens: bfloat16 [4, 512, 3584], P('pipe', 'expert', 'dp'), may hold values from -6 to 6
- expert_ids: int32 [4, 512, 2], P('pipe', 'expert'), may hold values from 0 to 3, all different within a row; in each aligned block of 128 rows (0 to 127, 128 to 255, ..., all dimensions but the last counted through in order) at most 128 rows name the same one
- gate_levels: int32 [4, 512, 2], P('pipe', 'expert'), may hold values from 1 to 255
- gain: bfloat16 [3584], P('dp'), may hold values from 0.5 to 2
- w_gate: bfloat16 [4, 3584, 1024], P('expert', None, 'dp'), may hold values from -0.09375 to 0.09375
- w_up: bfloat16 [4, 3584, 1024], P('expert', None, 'dp'), may hold values from -0.09375 to 0.09375
- w_down: bfloat16 [4, 1024, 3584], P('expert', 'dp'), may hold values from -0.1875 to 0.1875
Outputs:
- next_input: bfloat16 [4, 512, 3584], P('pipe', 'expert', 'dp')
The draws below stay inside these ranges and needn't reach their ends.
Inputs may be any that keep to these rules, and one draw needn't show every extreme that they name: `expert_ids`: each token names 2 different experts. Within each aligned block of 128 tokens of a section, no expert is named by more than 128 tokens, and in every draw some expert is named by exactly 128 tokens of some block.
All inputs are finite; a program needn't handle non-finite values.
Results may differ from the reference program's by a relative error of at most 0.012.
Values may be sent and summed in bfloat16 or wider, within the bound.
No kernel may reach another device: no remote copies, remote signals or barrier semaphores. Data moves between devices by JAX's collectives and lax.ppermute only.
A program may use at most 64 MiB of HBM per device.

```python
import math
import jax
import jax.numpy as jnp
import numpy as np
from jax import lax

D = 3584
FF = 1024
TOPW = 2
TOK_DEV = 128
EXPERTS = 4
TOKENS = 512
CAP = 128
N_PIPE = 4
N_DP = 2


def touch_ends(values, stream_key, low, largest):
    dims = values.shape
    place = [jax.random.randint(jax.random.fold_in(stream_key, axis), (), 0, dims[axis]) for axis in range(len(dims))]
    values = values.at[tuple(place)].set(low)
    longest = dims.index(max(dims))
    place[longest] = (place[longest] + 1) % dims[longest]
    return values.at[tuple(place)].set(largest)


def block_scale(stream_key, shape, cuts, low, top_value):
    def one(position, blocks):
        heights = jax.random.uniform(jax.random.fold_in(jax.random.fold_in(stream_key, 6), position), (blocks,), jnp.float32, low / len(cuts), top_value / len(cuts))
        return jnp.repeat(jnp.exp(heights), shape[position] // blocks).reshape((-1,) + (1,) * (len(shape) - position - 1))

    factor_of = one(*cuts[0])
    for cut in cuts[1:]:
        factor_of = factor_of * one(*cut)
    return factor_of


def deal_out(stream_key, own, number, rows, number_of, top, bound, lean):
    sequence = jax.random.permutation(stream_key, number_of)
    crowded, usual = load_shares(number_of, rows * top, bound, lean, True), load_shares(number_of, rows * top, bound, lean, False)
    places = jnp.arange(number_of)

    def named(sizes, rotation):
        used = int((sizes > 0).sum())
        fixed = max(1, used // 4)
        moved = fixed + (places - fixed + rotation * (used - fixed)) % max(1, number_of - fixed)
        return jnp.zeros((number_of,), jnp.int32).at[sequence[jnp.where(places < fixed, places, moved)]].set(jnp.asarray(sizes, jnp.int32))

    sizes = jnp.where(number % 4 == 0, named(crowded, number // 4), named(usual, number - number // 4 - 1))
    mixed = jax.random.permutation(jax.random.fold_in(own, 3), number_of)
    source_of, receiver = mixed[0:number_of // 2 * 2:2], mixed[1:number_of // 2 * 2:2]
    room = jnp.minimum(sizes[source_of] - 1, bound - sizes[receiver]) // 2
    room = jnp.where((source_of == sequence[0]) | (receiver == sequence[0]) | (sizes[receiver] == 0), 0, jnp.maximum(room, 0))
    moved = jax.random.randint(jax.random.fold_in(own, 4), (number_of // 2,), 0, 1 << 20) % (room + 1)
    sizes = sizes.at[source_of].add(-moved).at[receiver].add(moved)
    members = jnp.searchsorted(jnp.cumsum(sizes), jnp.arange(rows * top), side="right").astype(jnp.int32)
    grid = members.reshape(top, rows).T
    grid = grid[jax.random.permutation(jax.random.fold_in(own, 1), rows)]
    rotation = jax.random.randint(jax.random.fold_in(own, 2), (rows, 1), 0, top)
    return jnp.take_along_axis(grid, (jnp.arange(top)[None, :] + rotation) % top, axis=1)


def load_shares(number_of, total, most, slope, full):
    loads = [(1 << 20) // math.isqrt(standing ** slope) + 1 for standing in range(1, number_of + 1)]
    largest = most if full else min(most, max(-(-total // number_of), total * loads[0] // sum(loads)))
    least = 1 if total - largest >= number_of - 1 else 0
    counts, rest = [largest] + [least] * (number_of - 1), total - largest - least * (number_of - 1)
    while rest > 0:
        movable = [i for i in range(1, number_of) if counts[i] < largest] or [i for i in range(1, number_of) if counts[i] < most]
        pool, remaining = sum([loads[i] for i in movable]), rest
        for i in movable:
            more = min(most - counts[i], max(1, remaining * loads[i] // pool), rest)
            counts[i] = counts[i] + more
            rest = rest - more
    return np.array(counts)


def noise(rng, extent, deviation, most, cuts=(), kind=jnp.bfloat16):
    entries = jax.random.normal(rng, extent, jnp.float32) * deviation
    if len(cuts) > 0:
        entries = block_scale(rng, extent, cuts, -0.22, 0.18) * entries
    return jnp.clip(entries, min=-most, max=most).astype(kind)


def setup_inputs(seed: int = 0) -> dict:
    arg_keys = jax.random.split(jax.random.key(seed), 8)
    tokens = noise(arg_keys[0], (N_PIPE, TOKENS, D), 1.0, 6.0, ((0, 4), (1, 4), (2, 2)))
    expert_ids_keys = jax.random.split(jax.random.fold_in(arg_keys[1], 1), N_PIPE * TOKENS // TOK_DEV)
    expert_ids_turns = jax.random.permutation(jax.random.fold_in(arg_keys[1], 3), N_PIPE * TOKENS // TOK_DEV)
    expert_ids = jax.vmap(lambda own, number: deal_out(jax.random.fold_in(arg_keys[1], 2), own, number, TOK_DEV, EXPERTS, TOPW, CAP, 2))(expert_ids_keys, expert_ids_turns).reshape((N_PIPE, TOKENS, TOPW))
    gate_levels = touch_ends(jax.random.randint(arg_keys[2], (N_PIPE, TOKENS, TOPW), 1, 256), jax.random.fold_in(arg_keys[2], 1), 1, 255).astype(jnp.int32)
    gain = jnp.clip(jnp.exp(math.log(2.0) - 1.3862944 * jax.random.uniform(arg_keys[3], (D,), jnp.float32) ** block_scale(arg_keys[3], (D,), ((0, 2),), -0.2, 0.2)), 0.5, 2.0).astype(jnp.bfloat16)
    w_gate = noise(arg_keys[4], (EXPERTS, D, FF), D ** -0.5, 0.09375, ((0, 4), (2, 2)))
    w_up = noise(arg_keys[5], (EXPERTS, D, FF), D ** -0.5, 0.09375, ((0, 4), (2, 2)))
    w_down = noise(arg_keys[6], (EXPERTS, FF, D), FF ** -0.5, 0.1875, ((0, 4), (1, 2)))
    return {"tokens": tokens, "expert_ids": expert_ids, "gate_levels": gate_levels, "gain": gain, "w_gate": w_gate, "w_up": w_up, "w_down": w_down}


epsilon = 1e-06

def expert_block(rows, gain, weights_gate, weights_up, weights_down):
    wide_rows = rows.astype(jnp.float32)
    squares = lax.optimization_barrier(jnp.sum(jnp.square(wide_rows), axis=1))
    inverse = lax.rsqrt(squares / D + epsilon)
    scaled = (wide_rows * gain.astype(jnp.float32)[None, :]).astype(jnp.bfloat16)
    gate_value = inverse[:, None] * jnp.dot(scaled, weights_gate, preferred_element_type=jnp.float32)
    up_value = inverse[:, None] * jnp.dot(scaled, weights_up, preferred_element_type=jnp.float32)
    hidden = (jax.nn.silu(gate_value) * up_value).astype(jnp.bfloat16)
    quarter = FF // N_DP
    combined = jnp.zeros((rows.shape[0], D), jnp.float32)
    for portion in range(N_DP):
        partial_sum = jnp.dot(hidden[:, portion * quarter:(portion + 1) * quarter], weights_down[portion * quarter:(portion + 1) * quarter, :], preferred_element_type=jnp.float32).astype(jnp.bfloat16)
        partial_sum = lax.optimization_barrier(partial_sum)
        combined = combined + partial_sum.astype(jnp.float32)
    return combined.astype(jnp.bfloat16)

def reference(tokens, expert_ids, gate_levels, gain, w_gate, w_up, w_down):
    blocks = TOKENS // TOK_DEV
    limit = blocks * CAP
    token_iota = jnp.arange(TOKENS, dtype=jnp.int32)
    expert_iota = jnp.arange(EXPERTS, dtype=jnp.int32)

    def section_layer(item):
        rows_all, choose, levels = item
        matches = (choose[:, :, None] == expert_iota[None, None, :]).astype(jnp.int32)
        member = lax.optimization_barrier(jnp.sum(matches, axis=1)).astype(jnp.int32)
        blocked = member.reshape(blocks, TOK_DEV, EXPERTS)
        before = (jnp.cumsum(blocked, axis=1).astype(jnp.int32) - blocked).reshape(TOKENS, EXPERTS)
        slot_full = ((token_iota // TOK_DEV)[:, None] * CAP + before).astype(jnp.int32)
        target = jnp.where(member == 1, slot_full, limit).astype(jnp.int32)
        table = jnp.full((EXPERTS, limit), TOKENS, jnp.int32)
        table = table.at[jnp.broadcast_to(expert_iota[None, :], (TOKENS, EXPERTS)), target].set(jnp.broadcast_to(token_iota[:, None], (TOKENS, EXPERTS)), mode='drop')
        padded = jnp.concatenate([rows_all, jnp.zeros((1, D), jnp.bfloat16)], axis=0)

        def per_expert(pieces):
            index_row, gate_mat, up_mat, down_mat = pieces
            return expert_block(padded[index_row], gain, gate_mat, up_mat, down_mat)
        outputs = lax.map(per_expert, (table, w_gate, w_up, w_down))
        slot_pick = jnp.take_along_axis(slot_full, choose, axis=1).astype(jnp.int32)
        picked = outputs[choose, slot_pick]
        wide_levels = levels.astype(jnp.float32)
        shares = wide_levels / lax.optimization_barrier(jnp.sum(wide_levels, axis=1, keepdims=True))
        result = rows_all.astype(jnp.float32) + lax.optimization_barrier(jnp.sum(shares[:, :, None] * picked.astype(jnp.float32), axis=1))
        return result.astype(jnp.bfloat16)
    layer_out = lax.map(section_layer, (tokens, expert_ids, gate_levels))
    return jnp.roll(layer_out, 1, axis=0)
```

```python
import functools

import jax
import jax.numpy as jnp
from jax import lax
from jax.experimental import pallas as pl
from jax.experimental.pallas import tpu as pltpu
from jax.sharding import PartitionSpec as P

epsilon = 1e-06
LANES = 128


def from_behind(value, axis, by):
    size = lax.axis_size(axis)
    return lax.ppermute(value, axis, [(i, (i + by) % size) for i in range(size)])


def routed_body(tokens, expert_ids, gate_levels, gain, w_gate, w_up, w_down):
    own_rows = tokens[0]
    choose = expert_ids[0]
    levels = gate_levels[0].astype(jnp.float32)
    weights_gate = w_gate[0]
    weights_up = w_up[0]
    weights_down = w_down[0]
    num_tokens = own_rows.shape[0]
    quarter = own_rows.shape[1]
    fanout = choose.shape[1]
    experts = lax.axis_size("expert") * w_gate.shape[0]
    capacity = min(num_tokens, max(2, 2 * num_tokens * fanout // experts))
    full_width = weights_gate.shape[0]
    expert_iota = jnp.arange(experts, dtype=jnp.int32)
    matches = (choose[:, :, None] == expert_iota[None, None, :]).astype(jnp.int32)
    member = jnp.sum(matches, axis=1)
    before = jnp.cumsum(member, axis=0) - member
    slot_iota = jnp.arange(capacity, dtype=jnp.int32)
    placed = (member.T[:, None, :] == 1) & (before.T[:, None, :] == slot_iota[None, :, None])
    placed = placed.reshape(experts * capacity, num_tokens)
    outgoing = jnp.dot(placed.astype(jnp.bfloat16), own_rows, preferred_element_type=jnp.float32)
    outgoing = outgoing.astype(jnp.bfloat16).reshape(experts, capacity, quarter)
    slot_of = jnp.sum(
        matches * (expert_iota[None, None, :] * capacity + before[:, None, :]), axis=2
    )
    shares = levels / jnp.sum(levels, axis=1, keepdims=True)
    gain_row = gain[None, :]
    own_squares = jnp.sum(jnp.square(own_rows.astype(jnp.float32)), axis=1)
    row_total = lax.psum(own_squares, "dp")
    token_scale = lax.rsqrt(row_total / full_width + epsilon)
    slot_scales = jnp.sum(placed.astype(jnp.float32) * token_scale[None, :], axis=1).reshape(
        experts, capacity
    )
    arrived = lax.all_to_all(outgoing, "expert", split_axis=0, concat_axis=0, tiled=True)
    arrived_scale = lax.all_to_all(
        slot_scales.astype(jnp.bfloat16), "expert", split_axis=0, concat_axis=0, tiled=True
    ).astype(slot_scales.dtype)
    sources = arrived.shape[0]
    slot_count = arrived.shape[1]
    flat_rows = arrived.reshape(sources * slot_count, quarter)
    row_count = flat_rows.shape[0]
    part_rows = lax.all_gather(flat_rows, "dp", axis=1, tiled=True)
    part_gain = lax.all_gather(gain_row, "dp", axis=1, tiled=True)
    scaled = (part_rows.astype(jnp.float32) * part_gain.astype(jnp.float32)).astype(jnp.bfloat16)
    gate_acc = jnp.dot(scaled, weights_gate, preferred_element_type=jnp.float32)
    up_acc = jnp.dot(scaled, weights_up, preferred_element_type=jnp.float32)
    inverse = arrived_scale.reshape(row_count)
    gate_value = inverse[:, None] * gate_acc
    up_value = inverse[:, None] * up_acc
    hidden = (jax.nn.silu(gate_value) * up_value).astype(jnp.bfloat16)
    summed = lax.psum_scatter(
        lax.dot_general(
            weights_down, hidden, (((0,), (1,)), ((), ())), preferred_element_type=jnp.float32
        ).astype(jnp.bfloat16),
        "dp",
        scatter_dimension=0,
        tiled=True,
    )
    result = summed.reshape(quarter, sources, slot_count)
    returned_rows = lax.all_to_all(result, "expert", split_axis=1, concat_axis=1, tiled=True)
    flat_back = returned_rows.reshape(quarter, experts * capacity)
    every_slot = jnp.arange(experts * capacity, dtype=jnp.int32)
    combined = own_rows.astype(jnp.float32)
    for slot_pick in range(fanout):
        selector = (slot_of[:, slot_pick, None] == every_slot[None, :]).astype(jnp.bfloat16)
        picked = lax.dot_general(
            selector, flat_back, (((1,), (1,)), ((), ())), preferred_element_type=jnp.float32
        )
        combined = combined + shares[:, slot_pick, None] * picked
    layer_out = combined.astype(jnp.bfloat16)
    shifted = from_behind(layer_out, "pipe", 1)
    return shifted[None]


def plane_pairs(place):
    experts, halves = lax.axis_size("expert"), lax.axis_size("dp")
    pairs = []
    for expert in range(experts):
        for half in range(halves):
            row, member, other = place(expert // 2, expert % 2, half)
            pairs.append((expert * halves + half, (row * 2 + member) * halves + other))
    return pairs


def to_partner(value):
    return lax.ppermute(value, ("expert", "dp"), plane_pairs(lambda r, m, h: (r, 1 - m, h)))


def across(value, first):
    return lax.ppermute(
        value,
        ("expert", "dp"),
        plane_pairs(lambda r, m, h: (r, m, 1 - h) if (m == 0) == first else (1 - r, m, h)),
    )


def pack_kernel(rows_ref, gain_ref, ids_ref, levels_ref, *out_refs):
    chunk, width = out_refs[0].shape[0], rows_ref.shape[1]
    fanout = ids_ref.shape[1]
    gain = gain_ref[...].astype(jnp.float32)
    lane = lax.broadcasted_iota(jnp.int32, (chunk, LANES), 1)
    for part, out_ref in enumerate(out_refs):
        at = pl.ds(part * chunk, chunk)
        wide = rows_ref[at, :].astype(jnp.float32)
        out_ref[:, :width] = (wide * gain).astype(jnp.bfloat16)
        squares = jnp.sum(wide * wide, axis=1, keepdims=True)
        high = squares.astype(jnp.bfloat16).astype(jnp.float32)
        columns = [ids_ref[at, k : k + 1].astype(jnp.float32) for k in range(fanout)]
        columns += [levels_ref[at, k : k + 1].astype(jnp.float32) for k in range(fanout)]
        columns += [high, squares - high]
        packed = jnp.zeros((chunk, LANES), jnp.float32)
        for place, column in enumerate(columns):
            packed = jnp.where(lane == place, column, packed)
        out_ref[:, width:] = packed.astype(jnp.bfloat16)


def pack(rows, gain, ids, levels, parts):
    chunk, width = rows.shape[0] // parts, rows.shape[1]
    return pl.pallas_call(
        pack_kernel,
        out_shape=[jax.ShapeDtypeStruct((chunk, width + LANES), jnp.bfloat16)] * parts,
        in_specs=[pl.BlockSpec(memory_space=pltpu.VMEM)] * 4,
        out_specs=[pl.BlockSpec(memory_space=pltpu.VMEM)] * parts,
        name="pack",
    )(rows, gain, ids, levels)


def expert_kernel(fanout, place_ref, *refs):
    near, far = refs[:4], refs[4:8]
    gate_ref, up_ref, down_ref = refs[8:11]
    outs = refs[11:19]
    near_rows, far_rows, hidden_ref = refs[19:]
    chunk, width = near[0].shape[0], near_rows.shape[1]
    expert, half = place_ref[0], place_ref[1]
    near_at = pl.ds(pl.multiple_of(half * width, width), width)
    far_at = pl.ds(pl.multiple_of((1 - half) * width, width), width)
    for i in range(4):
        at = pl.ds(i * chunk, chunk)
        near_rows[at, :] = near[i][:, :width]
        far_rows[at, :] = far[i][:, :width]
    about = jnp.concatenate([r[:, width:] for r in near], axis=0).astype(jnp.float32)
    about_far = jnp.concatenate([r[:, width:] for r in far], axis=0).astype(jnp.float32)
    ss = about + about_far
    squares = ss[:, 2 * fanout : 2 * fanout + 1] + ss[:, 2 * fanout + 1 : 2 * fanout + 2]
    inverse = lax.rsqrt(squares / gate_ref.shape[0] + epsilon)
    total, mine = 0.0, 0.0
    for k in range(fanout):
        level = about[:, fanout + k : fanout + k + 1]
        total = total + level
        mine = mine + jnp.where(about[:, k : k + 1] == expert.astype(jnp.float32), level, 0.0)
    share = mine / total

    def product(w_ref, columns):
        return jnp.dot(
            near_rows[...], w_ref[near_at, columns], preferred_element_type=jnp.float32
        ) + jnp.dot(far_rows[...], w_ref[far_at, columns], preferred_element_type=jnp.float32)

    units = gate_ref.shape[1]
    step = min(units, 256)
    for start in range(0, units, step):
        columns = pl.ds(start, step)
        gate = inverse * product(gate_ref, columns)
        up = inverse * product(up_ref, columns)
        value = jnp.where(share > 0.0, jax.nn.silu(gate) * up * share, 0.0)
        hidden_ref[:, columns] = value.astype(jnp.bfloat16)
    hidden = hidden_ref[...]
    wide = 256 if width % 256 == 0 else width
    for side, base in ((1, 1 - half), (0, half)):
        for start in range(0, width, wide):
            columns = pl.ds(pl.multiple_of(base * width + start, 128), wide)
            value = jnp.dot(hidden, down_ref[:, columns], preferred_element_type=jnp.float32)
            value = value.astype(jnp.bfloat16)
            for i in range(4):
                outs[side * 4 + i][:, start : start + wide] = value[i * chunk : (i + 1) * chunk]


def expert_block(place, near, far, w_gate, w_up, w_down, fanout):
    chunk, width = near[0].shape[0], near[0].shape[1] - LANES
    vmem = pl.BlockSpec(memory_space=pltpu.VMEM)
    return pl.pallas_call(
        functools.partial(expert_kernel, fanout),
        out_shape=[jax.ShapeDtypeStruct((chunk, width), jnp.bfloat16)] * 8,
        in_specs=[pl.BlockSpec(memory_space=pltpu.SMEM)] + [vmem] * 11,
        out_specs=[vmem] * 8,
        scratch_shapes=[
            pltpu.VMEM((4 * chunk, width), jnp.bfloat16),
            pltpu.VMEM((4 * chunk, width), jnp.bfloat16),
            pltpu.VMEM((4 * chunk, w_gate.shape[1]), jnp.bfloat16),
        ],
        name="expert",
    )(place, *near, *far, w_gate, w_up, w_down)


def plus(*values):
    total = values[0].astype(jnp.float32)
    for value in values[1:]:
        total = total + value.astype(jnp.float32)
    return total


def dense_body(tokens, expert_ids, gate_levels, gain, w_gate, w_up, w_down):
    own_rows = tokens[0]
    parts = 2
    chunk = own_rows.shape[0] // parts
    fanout = expert_ids.shape[2]
    expert = lax.axis_index("expert")
    place = jnp.stack([expert, lax.axis_index("dp")]).astype(jnp.int32)
    first = expert % 2 == 0
    packed = pack(own_rows, gain[None, :], expert_ids[0], gate_levels[0], parts)
    results = []
    for part in range(parts):
        own = packed[part]
        one = across(own, True)
        two = across(own, False)
        diagonal = across(one, False)
        by_dp = jnp.where(first, one, two)
        by_row = jnp.where(first, two, one)
        near_mine = [own, by_row]
        far_mine = [by_dp, diagonal]
        near = near_mine + [to_partner(v) for v in near_mine]
        far = far_mine + [to_partner(v) for v in far_mine]
        outs = expert_block(place, near, far, w_gate[0], w_up[0], w_down[0], fanout)
        o_mine, r_mine, o_theirs, r_theirs, d_mine, dr_mine, d_theirs, dr_theirs = outs
        corner = plus(dr_mine, to_partner(dr_theirs)).astype(jnp.bfloat16)
        along_dp = plus(d_mine, to_partner(d_theirs))
        along_row = plus(r_mine, to_partner(r_theirs))
        stay = plus(o_mine, to_partner(o_theirs))
        got_corner = across(corner, True)
        second = jnp.where(first, along_dp, along_row).astype(jnp.bfloat16)
        got_second = across(second, True)
        third = jnp.where(first, along_row, along_dp) + got_corner.astype(jnp.float32)
        got_third = across(third.astype(jnp.bfloat16), False)
        kept = own_rows[part * chunk : (part + 1) * chunk]
        layer_out = plus(kept, stay, got_second, got_third).astype(jnp.bfloat16)
        results.append(from_behind(layer_out, "pipe", 1))
    return jnp.concatenate(results, axis=0)[None]


def solution(mesh):
    specs = dict(
        mesh=mesh,
        in_specs=(
            P("pipe", "expert", "dp"),
            P("pipe", "expert", None),
            P("pipe", "expert", None),
            P("dp"),
            P("expert", None, "dp"),
            P("expert", None, "dp"),
            P("expert", "dp", None),
        ),
        out_specs=P("pipe", "expert", "dp"),
        check_vma=False,
    )
    square = mesh.shape["expert"] == 4 and mesh.shape["dp"] == 2
    return jax.shard_map(dense_body if square else routed_body, **specs)
```

```python
import functools

import jax
import jax.numpy as jnp
from jax import lax
from jax.experimental import pallas as pl
from jax.experimental.pallas import tpu as pltpu
from jax.sharding import PartitionSpec as P


epsilon = 1e-06
LANES = 128
KERNEL_VMEM = 24 * 2**20


def from_behind(value, axis, by):
    size = lax.axis_size(axis)
    return lax.ppermute(value, axis, [(i, (i + by) % size) for i in range(size)])


def routed_body(tokens, expert_ids, gate_levels, gain, w_gate, w_up, w_down):
    own_rows = tokens[0]
    choose = expert_ids[0]
    levels = gate_levels[0].astype(jnp.float32)
    weights_gate = w_gate[0]
    weights_up = w_up[0]
    weights_down = w_down[0]
    num_tokens = own_rows.shape[0]
    quarter = own_rows.shape[1]
    fanout = choose.shape[1]
    experts = lax.axis_size("expert") * w_gate.shape[0]
    capacity = min(num_tokens, max(2, 2 * num_tokens * fanout // experts))
    full_width = weights_gate.shape[0]
    expert_iota = jnp.arange(experts, dtype=jnp.int32)
    matches = (choose[:, :, None] == expert_iota[None, None, :]).astype(jnp.int32)
    member = jnp.sum(matches, axis=1)
    before = jnp.cumsum(member, axis=0) - member
    slot_iota = jnp.arange(capacity, dtype=jnp.int32)
    placed = (member.T[:, None, :] == 1) & (before.T[:, None, :] == slot_iota[None, :, None])
    placed = placed.reshape(experts * capacity, num_tokens)
    outgoing = jnp.dot(placed.astype(jnp.bfloat16), own_rows, preferred_element_type=jnp.float32)
    outgoing = outgoing.astype(jnp.bfloat16).reshape(experts, capacity, quarter)
    slot_of = jnp.sum(
        matches * (expert_iota[None, None, :] * capacity + before[:, None, :]), axis=2
    )
    shares = levels / jnp.sum(levels, axis=1, keepdims=True)
    gain_row = gain[None, :]
    own_squares = jnp.sum(jnp.square(own_rows.astype(jnp.float32)), axis=1)
    row_total = lax.psum(own_squares, "dp")
    token_scale = lax.rsqrt(row_total / full_width + epsilon)
    slot_scales = jnp.sum(placed.astype(jnp.float32) * token_scale[None, :], axis=1).reshape(
        experts, capacity
    )
    arrived = lax.all_to_all(outgoing, "expert", split_axis=0, concat_axis=0, tiled=True)
    arrived_scale = lax.all_to_all(
        slot_scales.astype(jnp.bfloat16), "expert", split_axis=0, concat_axis=0, tiled=True
    ).astype(slot_scales.dtype)
    sources = arrived.shape[0]
    slot_count = arrived.shape[1]
    flat_rows = arrived.reshape(sources * slot_count, quarter)
    row_count = flat_rows.shape[0]
    part_rows = lax.all_gather(flat_rows, "dp", axis=1, tiled=True)
    part_gain = lax.all_gather(gain_row, "dp", axis=1, tiled=True)
    scaled = (part_rows.astype(jnp.float32) * part_gain.astype(jnp.float32)).astype(jnp.bfloat16)
    gate_acc = jnp.dot(scaled, weights_gate, preferred_element_type=jnp.float32)
    up_acc = jnp.dot(scaled, weights_up, preferred_element_type=jnp.float32)
    inverse = arrived_scale.reshape(row_count)
    gate_value = inverse[:, None] * gate_acc
    up_value = inverse[:, None] * up_acc
    hidden = (jax.nn.silu(gate_value) * up_value).astype(jnp.bfloat16)
    summed = lax.psum_scatter(
        lax.dot_general(
            weights_down, hidden, (((0,), (1,)), ((), ())), preferred_element_type=jnp.float32
        ).astype(jnp.bfloat16),
        "dp",
        scatter_dimension=0,
        tiled=True,
    )
    result = summed.reshape(quarter, sources, slot_count)
    returned_rows = lax.all_to_all(result, "expert", split_axis=1, concat_axis=1, tiled=True)
    flat_back = returned_rows.reshape(quarter, experts * capacity)
    every_slot = jnp.arange(experts * capacity, dtype=jnp.int32)
    combined = own_rows.astype(jnp.float32)
    for slot_pick in range(fanout):
        selector = (slot_of[:, slot_pick, None] == every_slot[None, :]).astype(jnp.bfloat16)
        picked = lax.dot_general(
            selector, flat_back, (((1,), (1,)), ((), ())), preferred_element_type=jnp.float32
        )
        combined = combined + shares[:, slot_pick, None] * picked
    layer_out = combined.astype(jnp.bfloat16)
    shifted = from_behind(layer_out, "pipe", 1)
    return shifted[None]


def plane_pairs(place):
    experts, halves = lax.axis_size("expert"), lax.axis_size("dp")
    pairs = []
    for expert in range(experts):
        for half in range(halves):
            row, member, other = place(expert // 2, expert % 2, half)
            pairs.append((expert * halves + half, (row * 2 + member) * halves + other))
    return pairs


def to_partner(value):
    return lax.ppermute(value, ("expert", "dp"), plane_pairs(lambda r, m, h: (r, 1 - m, h)))


def across(value, first):
    return lax.ppermute(
        value,
        ("expert", "dp"),
        plane_pairs(lambda r, m, h: (r, m, 1 - h) if (m == 0) == first else (1 - r, m, h)),
    )


def in_hbm():
    return pl.BlockSpec(memory_space=pltpu.HBM)


def in_vmem():
    return pl.BlockSpec(memory_space=pltpu.VMEM)


def pack_kernel(
    rows_hbm, gain_hbm, ids_hbm, levels_hbm, here_ref, kept_ref, away_ref, gain_out,
    rows_ref, gain_ref, ids_ref, levels_ref, sems,
):
    copies = [
        pltpu.make_async_copy(source, target, sems.at[i])
        for i, (source, target) in enumerate(
            ((ids_hbm, ids_ref), (levels_hbm, levels_ref), (gain_hbm, gain_ref), (rows_hbm, rows_ref))
        )
    ]
    for copy in copies:
        copy.start()
    width = rows_ref.shape[1]
    fanout, tokens = ids_ref.shape
    for copy in copies[:3]:
        copy.wait()
    gain_bits = gain_ref[...].reshape(1, width)
    gain = gain_bits.astype(jnp.float32)
    gain_out[...] = jnp.broadcast_to(gain_bits, gain_out.shape)
    about = jnp.concatenate(
        [
            ids_ref[...].astype(jnp.float32),
            levels_ref[...].astype(jnp.float32),
            jnp.zeros((LANES - 2 * fanout, tokens), jnp.float32),
        ],
        axis=0,
    ).T
    copies[3].wait()
    start = 0
    for out_ref in (here_ref, away_ref):
        chunk = out_ref.shape[0]
        raw = rows_ref[start : start + chunk, :]
        wide = raw.astype(jnp.float32)
        if out_ref is here_ref:
            out_ref[:, :width] = (wide * gain).astype(jnp.bfloat16)
            kept_ref[...] = raw
        else:
            out_ref[:, :width] = raw
        squares = jnp.sum(wide * wide, axis=1, keepdims=True)
        high = squares.astype(jnp.bfloat16).astype(jnp.float32)
        packed = about[start : start + chunk]
        lane = lax.broadcasted_iota(jnp.int32, packed.shape, 1)
        packed = jnp.where(lane == 2 * fanout, high, packed)
        packed = jnp.where(lane == 2 * fanout + 1, squares - high, packed)
        out_ref[:, width:] = packed.astype(jnp.bfloat16)
        start += chunk


def pack(rows, gain, ids, levels, here):
    tokens, width = rows.shape
    bf16 = functools.partial(jax.ShapeDtypeStruct, dtype=jnp.bfloat16)
    return pl.pallas_call(
        pack_kernel,
        out_shape=[
            bf16((here, width + LANES)), bf16((here, width)), bf16((tokens - here, width + LANES)),
            bf16((16, width)),
        ],
        in_specs=[in_hbm()] * 4,
        out_specs=[in_vmem()] * 4,
        scratch_shapes=[
            pltpu.VMEM(rows.shape, rows.dtype), pltpu.VMEM(gain.shape, gain.dtype),
            pltpu.VMEM(ids.shape, ids.dtype), pltpu.VMEM(levels.shape, levels.dtype),
            pltpu.SemaphoreType.DMA((4,)),
        ],
        compiler_params=pltpu.CompilerParams(vmem_limit_bytes=KERNEL_VMEM),
        name="pack",
    )(*[pltpu.with_memory_space_constraint(w, pltpu.HBM) for w in (rows, gain, ids, levels)])


def spread_kernel(row_ref, out_ref):
    out_ref[...] = jnp.broadcast_to(row_ref[:1], out_ref.shape)


def spread(row):
    return pl.pallas_call(
        spread_kernel,
        out_shape=jax.ShapeDtypeStruct((16, row.shape[1]), row.dtype),
        in_specs=[in_vmem()],
        out_specs=in_vmem(),
        compiler_params=pltpu.CompilerParams(vmem_limit_bytes=KERNEL_VMEM),
        cost_estimate=pl.CostEstimate(flops=2**32, bytes_accessed=0, transcendentals=0),
        name="spread",
    )(row)


def scale_kernel(rows_ref, gain_ref, out_ref):
    width = gain_ref.shape[1]
    gain = gain_ref[...].astype(jnp.float32)[:1]
    out_ref[:, :width] = (rows_ref[:, :width].astype(jnp.float32) * gain).astype(jnp.bfloat16)
    out_ref[:, width:] = rows_ref[:, width:]


def scale(rows, gain):
    return pl.pallas_call(
        scale_kernel,
        out_shape=jax.ShapeDtypeStruct(rows.shape, rows.dtype),
        in_specs=[in_vmem()] * 2,
        out_specs=in_vmem(),
        compiler_params=pltpu.CompilerParams(vmem_limit_bytes=KERNEL_VMEM),
        name="scale",
    )(rows, gain)


def half_columns(width):
    half = lax.axis_index("dp")
    return [pl.ds(pl.multiple_of(h * width, LANES), width) for h in (half, 1 - half)]


def dot(rows, weights):
    return jnp.dot(rows, weights, preferred_element_type=jnp.float32)


def early_kernel(fanout, *refs):
    own, one, two, own_p, one_p, two_p, gate_ref, up_ref = refs[:8]
    gate_acc, up_acc, facts_ref, near_rows, far_rows, near_about, far_about = refs[8:]
    chunk, width = own.shape[0], near_rows.shape[1]
    expert = lax.axis_index("expert")
    first = lax.rem(expert, 2) == 0
    near_at, far_at = half_columns(width)

    def fill(rows_ref, about_ref, pieces):
        for i, piece in enumerate(pieces):
            at = pl.ds(i * chunk, chunk)
            rows_ref[at, :] = piece[:, :width]
            about_ref[at, :] = piece[:, width:].astype(jnp.float32)

    @pl.when(first)
    def _():
        fill(near_rows, near_about, (own, own_p, two, one_p))
        fill(far_rows, far_about, (one, two_p))

    @pl.when(jnp.logical_not(first))
    def _():
        fill(near_rows, near_about, (own, own_p, one, two_p))
        fill(far_rows, far_about, (two, one_p))

    this = 2 * chunk
    step = min(gate_ref.shape[1], 256)
    for start in range(0, gate_ref.shape[1], step):
        columns = pl.ds(start, step)
        for weights, acc in ((gate_ref, gate_acc), (up_ref, up_acc)):
            near = dot(near_rows[...], weights[near_at, columns])
            acc[:this, columns] = near[:this] + dot(far_rows[...], weights[far_at, columns])
            acc[this:, columns] = near[this:]

    about = near_about[...]
    total, mine = 0.0, 0.0
    for k in range(fanout):
        level = about[:, fanout + k : fanout + k + 1]
        total = total + level
        mine = mine + jnp.where(about[:, k : k + 1] == expert.astype(jnp.float32), level, 0.0)
    place = 2 * fanout
    squares = about[:, place : place + 1] + about[:, place + 1 : place + 2]
    far = far_about[:, place : place + 1] + far_about[:, place + 1 : place + 2]
    lane = lax.broadcasted_iota(jnp.int32, (this, LANES), 1)
    share = mine / total
    facts_ref[:this, :] = jnp.where(lane == 0, share[:this], squares[:this] + far)
    facts_ref[this:, :] = jnp.where(lane == 0, share[this:], squares[this:])


def late_kernel(fanout, *refs):
    kept, corner, corner_p, gate_acc, up_acc, facts_ref, gate_ref, up_ref, down_ref = refs[:9]
    stay, corner_out, along, corner_p_out, along_p, stay_p = refs[9:15]
    corner_rows, hidden_ref = refs[15:]
    chunk, width = stay.shape
    this = 2 * chunk
    _, far_at = half_columns(width)
    corner_rows[:chunk, :] = corner[:, :width]
    corner_rows[chunk:, :] = corner_p[:, :width]
    place = 2 * fanout
    far = [
        about[:, place : place + 1] + about[:, place + 1 : place + 2]
        for about in [r[:, width:].astype(jnp.float32) for r in (corner, corner_p)]
    ]
    share, squares = facts_ref[:, :1], facts_ref[:, 1:2]
    squares = jnp.concatenate([squares[:this], squares[this:] + jnp.concatenate(far, axis=0)], axis=0)
    inverse = lax.rsqrt(squares / gate_ref.shape[0] + epsilon)
    step = min(gate_ref.shape[1], 256)
    for start in range(0, gate_ref.shape[1], step):
        columns = pl.ds(start, step)
        gate_corner = dot(corner_rows[...], gate_ref[far_at, columns])
        up_corner = dot(corner_rows[...], up_ref[far_at, columns])
        for at, gate_more, up_more in ((slice(0, this), 0.0, 0.0), (slice(this, None), gate_corner, up_corner)):
            gate = inverse[at] * (gate_acc[at, columns] + gate_more)
            up = inverse[at] * (up_acc[at, columns] + up_more)
            value = jnp.where(share[at] > 0.0, jax.nn.silu(gate) * up * share[at], 0.0)
            hidden_ref[at, columns] = value.astype(jnp.bfloat16)

    hidden = hidden_ref[...]
    wide = 256 if width % 256 == 0 else width
    role = lax.rem(lax.axis_index("expert"), 2)
    half = lax.axis_index("dp")
    for far_side in (True, False):
        for start in range(0, width, wide):
            at = pl.ds(start, wide)
            base = (1 - half if far_side else half) * width + start
            value = dot(hidden, down_ref[:, pl.ds(pl.multiple_of(base, LANES), wide)])
            here, here_p, other, other_p = [value[i * chunk : (i + 1) * chunk] for i in range(4)]
            if far_side:
                corner_out[:, at] = other.astype(jnp.bfloat16)
                corner_p_out[:, at] = other_p.astype(jnp.bfloat16)
                along[role, :, at] = here.astype(jnp.bfloat16)
                along_p[1 - role, :, at] = here_p.astype(jnp.bfloat16)
            else:
                stay[:, at] = kept[:, at].astype(jnp.float32) + here
                stay_p[:, at] = here_p.astype(jnp.bfloat16)
                along[1 - role, :, at] = other.astype(jnp.bfloat16)
                along_p[role, :, at] = other_p.astype(jnp.bfloat16)


def early_block(mine, theirs, w_gate, w_up, fanout):
    chunk, width = mine[0].shape[0], mine[0].shape[1] - LANES
    rows, units = 4 * chunk, w_gate.shape[1]
    f32 = functools.partial(jax.ShapeDtypeStruct, dtype=jnp.float32)
    return pl.pallas_call(
        functools.partial(early_kernel, fanout),
        out_shape=[f32((rows, units)), f32((rows, units)), f32((rows, LANES))],
        in_specs=[in_vmem()] * 8,
        out_specs=[in_vmem()] * 3,
        scratch_shapes=[
            pltpu.VMEM((rows, width), jnp.bfloat16),
            pltpu.VMEM((rows // 2, width), jnp.bfloat16),
            pltpu.VMEM((rows, LANES), jnp.float32),
            pltpu.VMEM((rows // 2, LANES), jnp.float32),
        ],
        compiler_params=pltpu.CompilerParams(vmem_limit_bytes=KERNEL_VMEM),
        cost_estimate=pl.CostEstimate(
            flops=3 * rows * w_gate.size, bytes_accessed=4 * w_gate.size, transcendentals=0
        ),
        name="early",
    )(*mine[:3], *theirs[:3], w_gate, w_up)


def late_block(kept, corner, corner_p, partial, w_gate, w_up, w_down, fanout):
    chunk, width = kept.shape[0], corner.shape[1] - LANES
    rows, units = 4 * chunk, w_gate.shape[1]
    piece = functools.partial(jax.ShapeDtypeStruct, dtype=jnp.bfloat16)
    one, two = piece((chunk, width)), piece((2, chunk, width))
    return pl.pallas_call(
        functools.partial(late_kernel, fanout),
        out_shape=[jax.ShapeDtypeStruct((chunk, width), jnp.float32), one, two, one, two, one],
        in_specs=[in_vmem()] * 9,
        out_specs=[in_vmem()] * 6,
        scratch_shapes=[
            pltpu.VMEM((rows // 2, width), jnp.bfloat16),
            pltpu.VMEM((rows, units), jnp.bfloat16),
        ],
        compiler_params=pltpu.CompilerParams(vmem_limit_bytes=KERNEL_VMEM),
        cost_estimate=pl.CostEstimate(
            flops=3 * rows * w_gate.size, bytes_accessed=6 * w_gate.size, transcendentals=0
        ),
        name="late",
    )(kept, corner, corner_p, *partial, w_gate, w_up, w_down)


def plus(*values):
    total = values[0].astype(jnp.float32)
    for value in values[1:]:
        total = total + value.astype(jnp.float32)
    return total.astype(jnp.bfloat16)


def dense_body(tokens, expert_ids, gate_levels, gain, w_gate, w_up, w_down):
    fanout = expert_ids.shape[2]
    here, kept, away, gain_rows = pack(
        tokens[0], gain, expert_ids[0].T, gate_levels[0].T, tokens.shape[1] // 2
    )
    gain_rows = spread(gain_rows)
    results = []
    for part in range(2):
        if part == 1:
            kept = from_behind(away, "pipe", 1)
            own = scale(kept, gain_rows)
        else:
            own = here
        one = across(own, True)
        two = across(own, False)
        corner = across(one, False)
        mine = [own, one, two, corner]
        theirs = [to_partner(v) for v in mine]
        weights = (w_gate[0], w_up[0], w_down[0])
        partial = early_block(mine, theirs, *weights[:2], fanout)
        outs = late_block(kept, mine[3], theirs[3], partial, *weights, fanout)
        stay, corner, along, corner_p, along_p, stay_p = outs
        corner = plus(corner, to_partner(corner_p))
        along_p = to_partner(along_p)
        second = plus(along[0], along_p[0])
        got_corner = across(corner, True)
        got_second = across(second, True)
        third = plus(along[1], along_p[1], got_corner)
        got_third = across(third, False)
        stay_p = to_partner(stay_p)
        out = plus(stay, stay_p, got_second, got_third)
        results.append(from_behind(out, "pipe", 1) if part == 0 else out)
    return jnp.concatenate(results, axis=0)[None]


def solution(mesh):
    specs = dict(
        mesh=mesh,
        in_specs=(
            P("pipe", "expert", "dp"),
            P("pipe", "expert", None),
            P("pipe", "expert", None),
            P("dp"),
            P("expert", None, "dp"),
            P("expert", None, "dp"),
            P("expert", "dp", None),
        ),
        out_specs=P("pipe", "expert", "dp"),
        check_vma=False,
    )
    if mesh.shape["expert"] == 4 and mesh.shape["dp"] == 2:
        return jax.shard_map(dense_body, **specs)
    return jax.shard_map(routed_body, **specs)
```

```python
import functools

import jax
import jax.numpy as jnp
from jax import lax
from jax.experimental import pallas as pl
from jax.experimental.pallas import tpu as pltpu
from jax.sharding import PartitionSpec as P


epsilon = 1e-06
LANES = 128
KERNEL_VMEM = 24 * 2**20


def from_behind(value, axis, by):
    size = lax.axis_size(axis)
    return lax.ppermute(value, axis, [(i, (i + by) % size) for i in range(size)])


def routed_body(tokens, expert_ids, gate_levels, gain, w_gate, w_up, w_down):
    own_rows = tokens[0]
    choose = expert_ids[0]
    levels = gate_levels[0].astype(jnp.float32)
    weights_gate = w_gate[0]
    weights_up = w_up[0]
    weights_down = w_down[0]
    num_tokens = own_rows.shape[0]
    quarter = own_rows.shape[1]
    fanout = choose.shape[1]
    experts = lax.axis_size("expert") * w_gate.shape[0]
    capacity = min(num_tokens, max(2, 2 * num_tokens * fanout // experts))
    full_width = weights_gate.shape[0]
    expert_iota = jnp.arange(experts, dtype=jnp.int32)
    matches = (choose[:, :, None] == expert_iota[None, None, :]).astype(jnp.int32)
    member = jnp.sum(matches, axis=1)
    before = jnp.cumsum(member, axis=0) - member
    slot_iota = jnp.arange(capacity, dtype=jnp.int32)
    placed = (member.T[:, None, :] == 1) & (before.T[:, None, :] == slot_iota[None, :, None])
    placed = placed.reshape(experts * capacity, num_tokens)
    outgoing = jnp.dot(placed.astype(jnp.bfloat16), own_rows, preferred_element_type=jnp.float32)
    outgoing = outgoing.astype(jnp.bfloat16).reshape(experts, capacity, quarter)
    slot_of = jnp.sum(
        matches * (expert_iota[None, None, :] * capacity + before[:, None, :]), axis=2
    )
    shares = levels / jnp.sum(levels, axis=1, keepdims=True)
    gain_row = gain[None, :]
    own_squares = jnp.sum(jnp.square(own_rows.astype(jnp.float32)), axis=1)
    row_total = lax.psum(own_squares, "dp")
    token_scale = lax.rsqrt(row_total / full_width + epsilon)
    slot_scales = jnp.sum(placed.astype(jnp.float32) * token_scale[None, :], axis=1).reshape(
        experts, capacity
    )
    arrived = lax.all_to_all(outgoing, "expert", split_axis=0, concat_axis=0, tiled=True)
    arrived_scale = lax.all_to_all(
        slot_scales.astype(jnp.bfloat16), "expert", split_axis=0, concat_axis=0, tiled=True
    ).astype(slot_scales.dtype)
    sources = arrived.shape[0]
    slot_count = arrived.shape[1]
    flat_rows = arrived.reshape(sources * slot_count, quarter)
    row_count = flat_rows.shape[0]
    part_rows = lax.all_gather(flat_rows, "dp", axis=1, tiled=True)
    part_gain = lax.all_gather(gain_row, "dp", axis=1, tiled=True)
    scaled = (part_rows.astype(jnp.float32) * part_gain.astype(jnp.float32)).astype(jnp.bfloat16)
    gate_acc = jnp.dot(scaled, weights_gate, preferred_element_type=jnp.float32)
    up_acc = jnp.dot(scaled, weights_up, preferred_element_type=jnp.float32)
    inverse = arrived_scale.reshape(row_count)
    gate_value = inverse[:, None] * gate_acc
    up_value = inverse[:, None] * up_acc
    hidden = (jax.nn.silu(gate_value) * up_value).astype(jnp.bfloat16)
    summed = lax.psum_scatter(
        lax.dot_general(
            weights_down, hidden, (((0,), (1,)), ((), ())), preferred_element_type=jnp.float32
        ).astype(jnp.bfloat16),
        "dp",
        scatter_dimension=0,
        tiled=True,
    )
    result = summed.reshape(quarter, sources, slot_count)
    returned_rows = lax.all_to_all(result, "expert", split_axis=1, concat_axis=1, tiled=True)
    flat_back = returned_rows.reshape(quarter, experts * capacity)
    every_slot = jnp.arange(experts * capacity, dtype=jnp.int32)
    combined = own_rows.astype(jnp.float32)
    for slot_pick in range(fanout):
        selector = (slot_of[:, slot_pick, None] == every_slot[None, :]).astype(jnp.bfloat16)
        picked = lax.dot_general(
            selector, flat_back, (((1,), (1,)), ((), ())), preferred_element_type=jnp.float32
        )
        combined = combined + shares[:, slot_pick, None] * picked
    layer_out = combined.astype(jnp.bfloat16)
    shifted = from_behind(layer_out, "pipe", 1)
    return shifted[None]


def plane_pairs(place):
    experts, halves = lax.axis_size("expert"), lax.axis_size("dp")
    pairs = []
    for expert in range(experts):
        for half in range(halves):
            row, member, other = place(expert // 2, expert % 2, half)
            pairs.append((expert * halves + half, (row * 2 + member) * halves + other))
    return pairs


def to_partner(value):
    return lax.ppermute(value, ("expert", "dp"), plane_pairs(lambda r, m, h: (r, 1 - m, h)))


def across(value, first):
    return lax.ppermute(
        value,
        ("expert", "dp"),
        plane_pairs(lambda r, m, h: (r, m, 1 - h) if (m == 0) == first else (1 - r, m, h)),
    )


def in_hbm():
    return pl.BlockSpec(memory_space=pltpu.HBM)


def in_vmem():
    return pl.BlockSpec(memory_space=pltpu.VMEM)


def pack_kernel(
    rows_hbm, gain_hbm, ids_hbm, levels_hbm, here_ref, kept_ref, away_ref, gain_out,
    rows_ref, gain_ref, ids_ref, levels_ref, sems,
):
    copies = [
        pltpu.make_async_copy(source, target, sems.at[i])
        for i, (source, target) in enumerate(
            ((ids_hbm, ids_ref), (levels_hbm, levels_ref), (gain_hbm, gain_ref), (rows_hbm, rows_ref))
        )
    ]
    for copy in copies:
        copy.start()
    width = rows_ref.shape[1]
    fanout, tokens = ids_ref.shape
    for copy in copies[:3]:
        copy.wait()
    gain_bits = gain_ref[...].reshape(1, width)
    gain = gain_bits.astype(jnp.float32)
    gain_out[...] = jnp.broadcast_to(gain_bits, gain_out.shape)
    about = jnp.concatenate(
        [
            ids_ref[...].astype(jnp.float32),
            levels_ref[...].astype(jnp.float32),
            jnp.zeros((LANES - 2 * fanout, tokens), jnp.float32),
        ],
        axis=0,
    ).T
    copies[3].wait()
    start = 0
    for out_ref in (here_ref, away_ref):
        chunk = out_ref.shape[0]
        raw = rows_ref[start : start + chunk, :]
        wide = raw.astype(jnp.float32)
        if out_ref is here_ref:
            out_ref[:, :width] = (wide * gain).astype(jnp.bfloat16)
            kept_ref[...] = raw
        else:
            out_ref[:, :width] = raw
        squares = jnp.sum(wide * wide, axis=1, keepdims=True)
        high = squares.astype(jnp.bfloat16).astype(jnp.float32)
        packed = about[start : start + chunk]
        lane = lax.broadcasted_iota(jnp.int32, packed.shape, 1)
        packed = jnp.where(lane == 2 * fanout, high, packed)
        packed = jnp.where(lane == 2 * fanout + 1, squares - high, packed)
        out_ref[:, width:] = packed.astype(jnp.bfloat16)
        start += chunk


def pack(rows, gain, ids, levels, here):
    tokens, width = rows.shape
    bf16 = functools.partial(jax.ShapeDtypeStruct, dtype=jnp.bfloat16)
    return pl.pallas_call(
        pack_kernel,
        out_shape=[
            bf16((here, width + LANES)), bf16((here, width)), bf16((tokens - here, width + LANES)),
            bf16((16, width)),
        ],
        in_specs=[in_hbm()] * 4,
        out_specs=[in_vmem()] * 4,
        scratch_shapes=[
            pltpu.VMEM(rows.shape, rows.dtype), pltpu.VMEM(gain.shape, gain.dtype),
            pltpu.VMEM(ids.shape, ids.dtype), pltpu.VMEM(levels.shape, levels.dtype),
            pltpu.SemaphoreType.DMA((4,)),
        ],
        compiler_params=pltpu.CompilerParams(vmem_limit_bytes=KERNEL_VMEM),
        name="pack",
    )(*[pltpu.with_memory_space_constraint(w, pltpu.HBM) for w in (rows, gain, ids, levels)])


def spread_kernel(row_ref, out_ref):
    out_ref[...] = jnp.broadcast_to(row_ref[:1], out_ref.shape)


def spread(row):
    return pl.pallas_call(
        spread_kernel,
        out_shape=jax.ShapeDtypeStruct((16, row.shape[1]), row.dtype),
        in_specs=[in_vmem()],
        out_specs=in_vmem(),
        compiler_params=pltpu.CompilerParams(vmem_limit_bytes=KERNEL_VMEM),
        cost_estimate=pl.CostEstimate(flops=2**32, bytes_accessed=0, transcendentals=0),
        name="spread",
    )(row)


def scale_kernel(rows_ref, gain_ref, out_ref):
    width = gain_ref.shape[1]
    gain = gain_ref[...].astype(jnp.float32)[:1]
    out_ref[:, :width] = (rows_ref[:, :width].astype(jnp.float32) * gain).astype(jnp.bfloat16)
    out_ref[:, width:] = rows_ref[:, width:]


def scale(rows, gain):
    return pl.pallas_call(
        scale_kernel,
        out_shape=jax.ShapeDtypeStruct(rows.shape, rows.dtype),
        in_specs=[in_vmem()] * 2,
        out_specs=in_vmem(),
        compiler_params=pltpu.CompilerParams(vmem_limit_bytes=KERNEL_VMEM),
        name="scale",
    )(rows, gain)


def half_columns(width):
    half = lax.axis_index("dp")
    return [pl.ds(pl.multiple_of(h * width, LANES), width) for h in (half, 1 - half)]


def dot(rows, weights):
    return jnp.dot(rows, weights, preferred_element_type=jnp.float32)


def early_kernel(fanout, *refs):
    own, one, two, own_p, one_p, two_p, gate_ref, up_ref = refs[:8]
    gate_acc, up_acc, facts_ref, near_rows, far_rows, near_about, far_about = refs[8:]
    chunk, width = own.shape[0], near_rows.shape[1]
    expert = lax.axis_index("expert")
    first = lax.rem(expert, 2) == 0
    near_at, far_at = half_columns(width)

    def fill(rows_ref, about_ref, pieces):
        for i, piece in enumerate(pieces):
            at = pl.ds(i * chunk, chunk)
            rows_ref[at, :] = piece[:, :width]
            about_ref[at, :] = piece[:, width:].astype(jnp.float32)

    @pl.when(first)
    def _():
        fill(near_rows, near_about, (own, own_p, two, one_p))
        fill(far_rows, far_about, (one, two_p))

    @pl.when(jnp.logical_not(first))
    def _():
        fill(near_rows, near_about, (own, own_p, one, two_p))
        fill(far_rows, far_about, (two, one_p))

    this = 2 * chunk
    step = min(gate_ref.shape[1], 256)
    for start in range(0, gate_ref.shape[1], step):
        columns = pl.ds(start, step)
        for weights, acc in ((gate_ref, gate_acc), (up_ref, up_acc)):
            near = dot(near_rows[...], weights[near_at, columns])
            acc[:this, columns] = near[:this] + dot(far_rows[...], weights[far_at, columns])
            acc[this:, columns] = near[this:]

    about = near_about[...]
    total, mine = 0.0, 0.0
    for k in range(fanout):
        level = about[:, fanout + k : fanout + k + 1]
        total = total + level
        mine = mine + jnp.where(about[:, k : k + 1] == expert.astype(jnp.float32), level, 0.0)
    place = 2 * fanout
    squares = about[:, place : place + 1] + about[:, place + 1 : place + 2]
    far = far_about[:, place : place + 1] + far_about[:, place + 1 : place + 2]
    lane = lax.broadcasted_iota(jnp.int32, (this, LANES), 1)
    share = mine / total
    facts_ref[:this, :] = jnp.where(lane == 0, share[:this], squares[:this] + far)
    facts_ref[this:, :] = jnp.where(lane == 0, share[this:], squares[this:])


def down_product(hidden_ref, down_ref, far_side, width, store):
    hidden = hidden_ref[...]
    chunk = hidden.shape[0] // 4
    half = lax.axis_index("dp")
    wide = 256 if width % 256 == 0 else width
    for start in range(0, width, wide):
        base = (1 - half if far_side else half) * width + start
        value = dot(hidden, down_ref[:, pl.ds(pl.multiple_of(base, LANES), wide)])
        store(pl.ds(start, wide), *[value[i * chunk : (i + 1) * chunk] for i in range(4)])


def late_kernel(fanout, *refs):
    corner, corner_p, gate_acc, up_acc, facts_ref, gate_ref, up_ref, down_ref = refs[:8]
    hidden_ref, corner_out, corner_p_out, far_out, far_p_out, corner_rows = refs[8:]
    chunk, width = corner_out.shape
    this = 2 * chunk
    far_at = half_columns(width)[1]
    corner_rows[:chunk, :] = corner[:, :width]
    corner_rows[chunk:, :] = corner_p[:, :width]
    place = 2 * fanout
    far = [
        about[:, place : place + 1] + about[:, place + 1 : place + 2]
        for about in [r[:, width:].astype(jnp.float32) for r in (corner, corner_p)]
    ]
    share, squares = facts_ref[:, :1], facts_ref[:, 1:2]
    squares = jnp.concatenate([squares[:this], squares[this:] + jnp.concatenate(far, axis=0)], axis=0)
    inverse = lax.rsqrt(squares / gate_ref.shape[0] + epsilon)
    step = min(gate_ref.shape[1], 256)
    for start in range(0, gate_ref.shape[1], step):
        columns = pl.ds(start, step)
        gate_corner = dot(corner_rows[...], gate_ref[far_at, columns])
        up_corner = dot(corner_rows[...], up_ref[far_at, columns])
        for at, gate_more, up_more in ((slice(0, this), 0.0, 0.0), (slice(this, None), gate_corner, up_corner)):
            gate = inverse[at] * (gate_acc[at, columns] + gate_more)
            up = inverse[at] * (up_acc[at, columns] + up_more)
            value = jnp.where(share[at] > 0.0, jax.nn.silu(gate) * up * share[at], 0.0)
            hidden_ref[at, columns] = value.astype(jnp.bfloat16)

    def store(at, here, here_p, other, other_p):
        corner_out[:, at] = other.astype(jnp.bfloat16)
        corner_p_out[:, at] = other_p.astype(jnp.bfloat16)
        far_out[:, at] = here.astype(jnp.bfloat16)
        far_p_out[:, at] = here_p.astype(jnp.bfloat16)

    down_product(hidden_ref, down_ref, True, width, store)


def last_kernel(kept, hidden_ref, far, far_p, down_ref, stay, along, along_p, stay_p):
    role = lax.rem(lax.axis_index("expert"), 2)
    along[role, :, :] = far[...]
    along_p[1 - role, :, :] = far_p[...]

    def store(at, here, here_p, other, other_p):
        stay[:, at] = kept[:, at].astype(jnp.float32) + here
        stay_p[:, at] = here_p.astype(jnp.bfloat16)
        along[1 - role, :, at] = other.astype(jnp.bfloat16)
        along_p[role, :, at] = other_p.astype(jnp.bfloat16)

    down_product(hidden_ref, down_ref, False, stay.shape[1], store)


def join_kernel(moved, stay, stay_p, second, third, out_hbm, sum_ref, sems):
    chunk = moved.shape[0]
    first = pltpu.make_async_copy(moved, out_hbm.at[pl.ds(0, chunk), :], sems.at[0])
    first.start()
    total = stay[...] + stay_p[...].astype(jnp.float32)
    total = total + second[...].astype(jnp.float32) + third[...].astype(jnp.float32)
    sum_ref[...] = total.astype(jnp.bfloat16)
    rest = pltpu.make_async_copy(sum_ref, out_hbm.at[pl.ds(chunk, sum_ref.shape[0]), :], sems.at[1])
    rest.start()
    first.wait()
    rest.wait()


def join(moved, stay, *pieces):
    rows, width = stay.shape
    return pl.pallas_call(
        join_kernel,
        out_shape=jax.ShapeDtypeStruct((moved.shape[0] + rows, width), jnp.bfloat16),
        in_specs=[in_vmem()] * 5,
        out_specs=in_hbm(),
        scratch_shapes=[pltpu.VMEM((rows, width), jnp.bfloat16), pltpu.SemaphoreType.DMA((2,))],
        compiler_params=pltpu.CompilerParams(vmem_limit_bytes=KERNEL_VMEM),
        name="join",
    )(moved, stay, *pieces)


def early_block(mine, theirs, w_gate, w_up, fanout):
    chunk, width = mine[0].shape[0], mine[0].shape[1] - LANES
    rows, units = 4 * chunk, w_gate.shape[1]
    f32 = functools.partial(jax.ShapeDtypeStruct, dtype=jnp.float32)
    return pl.pallas_call(
        functools.partial(early_kernel, fanout),
        out_shape=[f32((rows, units)), f32((rows, units)), f32((rows, LANES))],
        in_specs=[in_vmem()] * 8,
        out_specs=[in_vmem()] * 3,
        scratch_shapes=[
            pltpu.VMEM((rows, width), jnp.bfloat16),
            pltpu.VMEM((rows // 2, width), jnp.bfloat16),
            pltpu.VMEM((rows, LANES), jnp.float32),
            pltpu.VMEM((rows // 2, LANES), jnp.float32),
        ],
        compiler_params=pltpu.CompilerParams(vmem_limit_bytes=KERNEL_VMEM),
        cost_estimate=pl.CostEstimate(
            flops=3 * rows * w_gate.size, bytes_accessed=4 * w_gate.size, transcendentals=0
        ),
        name="early",
    )(*mine[:3], *theirs[:3], w_gate, w_up)


def late_block(corner, corner_p, partial, w_gate, w_up, w_down, fanout):
    chunk, width = corner.shape[0], corner.shape[1] - LANES
    rows, units = 4 * chunk, w_gate.shape[1]
    piece = functools.partial(jax.ShapeDtypeStruct, dtype=jnp.bfloat16)
    return pl.pallas_call(
        functools.partial(late_kernel, fanout),
        out_shape=[piece((rows, units))] + [piece((chunk, width))] * 4,
        in_specs=[in_vmem()] * 8,
        out_specs=[in_vmem()] * 5,
        scratch_shapes=[pltpu.VMEM((rows // 2, width), jnp.bfloat16)],
        compiler_params=pltpu.CompilerParams(vmem_limit_bytes=KERNEL_VMEM),
        cost_estimate=pl.CostEstimate(
            flops=2 * rows * w_gate.size, bytes_accessed=5 * w_gate.size, transcendentals=0
        ),
        name="late",
    )(corner, corner_p, *partial, w_gate, w_up, w_down)


def last_block(kept, hidden, far, far_p, w_down):
    chunk, width = far.shape
    piece = functools.partial(jax.ShapeDtypeStruct, dtype=jnp.bfloat16)
    two = piece((2, chunk, width))
    return pl.pallas_call(
        last_kernel,
        out_shape=[jax.ShapeDtypeStruct((chunk, width), jnp.float32), two, two, piece((chunk, width))],
        in_specs=[in_vmem()] * 5,
        out_specs=[in_vmem()] * 4,
        compiler_params=pltpu.CompilerParams(vmem_limit_bytes=KERNEL_VMEM),
        cost_estimate=pl.CostEstimate(
            flops=4 * chunk * w_down.size, bytes_accessed=w_down.size, transcendentals=0
        ),
        name="last",
    )(kept, hidden, far, far_p, w_down)


def plus(*values):
    total = values[0].astype(jnp.float32)
    for value in values[1:]:
        total = total + value.astype(jnp.float32)
    return total.astype(jnp.bfloat16)


def dense_body(tokens, expert_ids, gate_levels, gain, w_gate, w_up, w_down):
    fanout = expert_ids.shape[2]
    here, kept, away, gain_rows = pack(
        tokens[0], gain, expert_ids[0].T, gate_levels[0].T, tokens.shape[1] // 2
    )
    gain_rows = spread(gain_rows)
    for part in range(2):
        if part == 1:
            kept = from_behind(away, "pipe", 1)
            own = scale(kept, gain_rows)
        else:
            own = here
        one = across(own, True)
        two = across(own, False)
        corner = across(one, False)
        mine = [own, one, two, corner]
        theirs = [to_partner(v) for v in mine]
        weights = (w_gate[0], w_up[0], w_down[0])
        partial = early_block(mine, theirs, *weights[:2], fanout)
        hidden, corner, corner_p, far, far_p = late_block(
            mine[3], theirs[3], partial, *weights, fanout
        )
        corner_p = to_partner(corner_p)
        stay, along, along_p, stay_p = last_block(kept, hidden, far, far_p, weights[2])
        corner = plus(corner, corner_p)
        along_p = to_partner(along_p)
        second = plus(along[0], along_p[0])
        got_corner = across(corner, True)
        got_second = across(second, True)
        third = plus(along[1], along_p[1], got_corner)
        got_third = across(third, False)
        stay_p = to_partner(stay_p)
        if part == 0:
            out = plus(stay, stay_p, got_second, got_third)
            moved = from_behind(out, "pipe", 1)
        else:
            out = join(moved, stay, stay_p, got_second, got_third)
    return out[None]


def solution(mesh):
    specs = dict(
        mesh=mesh,
        in_specs=(
            P("pipe", "expert", "dp"),
            P("pipe", "expert", None),
            P("pipe", "expert", None),
            P("dp"),
            P("expert", None, "dp"),
            P("expert", None, "dp"),
            P("expert", "dp", None),
        ),
        out_specs=P("pipe", "expert", "dp"),
        check_vma=False,
    )
    if mesh.shape["expert"] == 4 and mesh.shape["dp"] == 2:
        return jax.shard_map(dense_body, **specs)
    return jax.shard_map(routed_body, **specs)
```

```python
import functools

import jax
import jax.numpy as jnp
from jax import lax
from jax.experimental import pallas as pl
from jax.experimental.pallas import tpu as pltpu
from jax.sharding import PartitionSpec as P


epsilon = 1e-06
LANES = 128
FACTS = 16
KERNEL_VMEM = 24 * 2**20


def from_behind(value, axis, by):
    size = lax.axis_size(axis)
    return lax.ppermute(value, axis, [(i, (i + by) % size) for i in range(size)])


def routed_body(tokens, expert_ids, gate_levels, gain, w_gate, w_up, w_down):
    own_rows = tokens[0]
    choose = expert_ids[0]
    levels = gate_levels[0].astype(jnp.float32)
    weights_gate = w_gate[0]
    weights_up = w_up[0]
    weights_down = w_down[0]
    num_tokens = own_rows.shape[0]
    quarter = own_rows.shape[1]
    fanout = choose.shape[1]
    experts = lax.axis_size("expert") * w_gate.shape[0]
    capacity = min(num_tokens, max(2, 2 * num_tokens * fanout // experts))
    full_width = weights_gate.shape[0]
    expert_iota = jnp.arange(experts, dtype=jnp.int32)
    matches = (choose[:, :, None] == expert_iota[None, None, :]).astype(jnp.int32)
    member = jnp.sum(matches, axis=1)
    before = jnp.cumsum(member, axis=0) - member
    slot_iota = jnp.arange(capacity, dtype=jnp.int32)
    placed = (member.T[:, None, :] == 1) & (before.T[:, None, :] == slot_iota[None, :, None])
    placed = placed.reshape(experts * capacity, num_tokens)
    outgoing = jnp.dot(placed.astype(jnp.bfloat16), own_rows, preferred_element_type=jnp.float32)
    outgoing = outgoing.astype(jnp.bfloat16).reshape(experts, capacity, quarter)
    slot_of = jnp.sum(
        matches * (expert_iota[None, None, :] * capacity + before[:, None, :]), axis=2
    )
    shares = levels / jnp.sum(levels, axis=1, keepdims=True)
    gain_row = gain[None, :]
    own_squares = jnp.sum(jnp.square(own_rows.astype(jnp.float32)), axis=1)
    row_total = lax.psum(own_squares, "dp")
    token_scale = lax.rsqrt(row_total / full_width + epsilon)
    slot_scales = jnp.sum(placed.astype(jnp.float32) * token_scale[None, :], axis=1).reshape(
        experts, capacity
    )
    arrived = lax.all_to_all(outgoing, "expert", split_axis=0, concat_axis=0, tiled=True)
    arrived_scale = lax.all_to_all(
        slot_scales.astype(jnp.bfloat16), "expert", split_axis=0, concat_axis=0, tiled=True
    ).astype(slot_scales.dtype)
    sources = arrived.shape[0]
    slot_count = arrived.shape[1]
    flat_rows = arrived.reshape(sources * slot_count, quarter)
    row_count = flat_rows.shape[0]
    part_rows = lax.all_gather(flat_rows, "dp", axis=1, tiled=True)
    part_gain = lax.all_gather(gain_row, "dp", axis=1, tiled=True)
    scaled = (part_rows.astype(jnp.float32) * part_gain.astype(jnp.float32)).astype(jnp.bfloat16)
    gate_acc = jnp.dot(scaled, weights_gate, preferred_element_type=jnp.float32)
    up_acc = jnp.dot(scaled, weights_up, preferred_element_type=jnp.float32)
    inverse = arrived_scale.reshape(row_count)
    gate_value = inverse[:, None] * gate_acc
    up_value = inverse[:, None] * up_acc
    hidden = (jax.nn.silu(gate_value) * up_value).astype(jnp.bfloat16)
    summed = lax.psum_scatter(
        lax.dot_general(
            weights_down, hidden, (((0,), (1,)), ((), ())), preferred_element_type=jnp.float32
        ).astype(jnp.bfloat16),
        "dp",
        scatter_dimension=0,
        tiled=True,
    )
    result = summed.reshape(quarter, sources, slot_count)
    returned_rows = lax.all_to_all(result, "expert", split_axis=1, concat_axis=1, tiled=True)
    flat_back = returned_rows.reshape(quarter, experts * capacity)
    every_slot = jnp.arange(experts * capacity, dtype=jnp.int32)
    combined = own_rows.astype(jnp.float32)
    for slot_pick in range(fanout):
        selector = (slot_of[:, slot_pick, None] == every_slot[None, :]).astype(jnp.bfloat16)
        picked = lax.dot_general(
            selector, flat_back, (((1,), (1,)), ((), ())), preferred_element_type=jnp.float32
        )
        combined = combined + shares[:, slot_pick, None] * picked
    layer_out = combined.astype(jnp.bfloat16)
    shifted = from_behind(layer_out, "pipe", 1)
    return shifted[None]


def plane_pairs(place):
    experts, halves = lax.axis_size("expert"), lax.axis_size("dp")
    pairs = []
    for expert in range(experts):
        for half in range(halves):
            row, member, other = place(expert // 2, expert % 2, half)
            pairs.append((expert * halves + half, (row * 2 + member) * halves + other))
    return pairs


def to_partner(value):
    return lax.ppermute(value, ("expert", "dp"), plane_pairs(lambda r, m, h: (r, 1 - m, h)))


def across(value, first):
    return lax.ppermute(
        value,
        ("expert", "dp"),
        plane_pairs(lambda r, m, h: (r, m, 1 - h) if (m == 0) == first else (1 - r, m, h)),
    )


def in_hbm():
    return pl.BlockSpec(memory_space=pltpu.HBM)


def in_vmem():
    return pl.BlockSpec(memory_space=pltpu.VMEM)


def tiles(chunk, width):
    return [
        (slice(k * chunk, (k + 1) * chunk), slice(k * LANES, (k + 1) * LANES))
        for k in range(width // LANES)
    ]


def piece_rows(chunk, width):
    return chunk * width // LANES


def pack_kernel(
    rows_hbm, gain_hbm, ids_hbm, levels_hbm, here_ref, kept_ref, away_ref, gain_out,
    rows_ref, gain_ref, ids_ref, levels_ref, sems,
):
    copies = [
        pltpu.make_async_copy(source, target, sems.at[i])
        for i, (source, target) in enumerate(
            ((ids_hbm, ids_ref), (levels_hbm, levels_ref), (gain_hbm, gain_ref), (rows_hbm, rows_ref))
        )
    ]
    for copy in copies:
        copy.start()
    width = rows_ref.shape[1]
    fanout, _ = ids_ref.shape
    for copy in copies[:3]:
        copy.wait()
    gain_bits = gain_ref[...].reshape(1, width)
    gain = gain_bits.astype(jnp.float32)
    gain_out[...] = jnp.broadcast_to(gain_bits, gain_out.shape)
    copies[3].wait()
    start = 0
    for out_ref in (here_ref, away_ref):
        chunk = (out_ref.shape[0] - FACTS) * LANES // width
        wide = rows_ref[start : start + chunk, :].astype(jnp.float32)
        for at, columns in tiles(chunk, width):
            if out_ref is here_ref:
                kept_ref[at, :] = rows_ref[start : start + chunk, columns]
                out_ref[at, :] = (wide[:, columns] * gain[:, columns]).astype(jnp.bfloat16)
            else:
                out_ref[at, :] = rows_ref[start : start + chunk, columns]
        lane = lax.broadcasted_iota(jnp.int32, (chunk, LANES), 1)
        token = lax.broadcasted_iota(jnp.int32, (chunk, LANES), 0) + start
        squares = jnp.sum(wide * wide, axis=1, keepdims=True)
        squares = jnp.sum(jnp.where(lane == token, squares, 0.0), axis=0, keepdims=True)
        high = squares.astype(jnp.bfloat16).astype(jnp.float32)
        lines = [ids_ref[k : k + 1, :].astype(jnp.float32) for k in range(fanout)]
        lines += [levels_ref[k : k + 1, :].astype(jnp.float32) for k in range(fanout)]
        facts = jnp.zeros((FACTS, LANES), jnp.float32)
        row = lax.broadcasted_iota(jnp.int32, facts.shape, 0)
        for k, line in enumerate(lines + [high, squares - high]):
            facts = jnp.where(row == k, line, facts)
        out_ref[out_ref.shape[0] - FACTS :, :] = facts.astype(jnp.bfloat16)
        start += chunk


def pack(rows, gain, ids, levels, here):
    tokens, width = rows.shape
    bf16 = functools.partial(jax.ShapeDtypeStruct, dtype=jnp.bfloat16)
    return pl.pallas_call(
        pack_kernel,
        out_shape=[
            bf16((piece_rows(here, width) + FACTS, LANES)), bf16((piece_rows(here, width), LANES)),
            bf16((piece_rows(tokens - here, width) + FACTS, LANES)),
            bf16((16, width)),
        ],
        in_specs=[in_hbm()] * 4,
        out_specs=[in_vmem()] * 4,
        scratch_shapes=[
            pltpu.VMEM(rows.shape, rows.dtype), pltpu.VMEM(gain.shape, gain.dtype),
            pltpu.VMEM(ids.shape, ids.dtype), pltpu.VMEM(levels.shape, levels.dtype),
            pltpu.SemaphoreType.DMA((4,)),
        ],
        compiler_params=pltpu.CompilerParams(vmem_limit_bytes=KERNEL_VMEM),
        name="pack",
    )(*[pltpu.with_memory_space_constraint(w, pltpu.HBM) for w in (rows, gain, ids, levels)])


def spread_kernel(row_ref, out_ref):
    out_ref[...] = jnp.broadcast_to(row_ref[:1], out_ref.shape)


def spread(row):
    return pl.pallas_call(
        spread_kernel,
        out_shape=jax.ShapeDtypeStruct((16, row.shape[1]), row.dtype),
        in_specs=[in_vmem()],
        out_specs=in_vmem(),
        compiler_params=pltpu.CompilerParams(vmem_limit_bytes=KERNEL_VMEM),
        cost_estimate=pl.CostEstimate(flops=2**32, bytes_accessed=0, transcendentals=0),
        name="spread",
    )(row)


def scale_kernel(rows_ref, gain_ref, out_ref):
    width = gain_ref.shape[1]
    body = rows_ref.shape[0] - FACTS
    gain = gain_ref[...].astype(jnp.float32)[:1]
    for at, columns in tiles(body * LANES // width, width):
        out_ref[at, :] = (rows_ref[at, :].astype(jnp.float32) * gain[:, columns]).astype(jnp.bfloat16)
    out_ref[body:, :] = rows_ref[body:, :]


def scale(rows, gain):
    return pl.pallas_call(
        scale_kernel,
        out_shape=jax.ShapeDtypeStruct(rows.shape, rows.dtype),
        in_specs=[in_vmem()] * 2,
        out_specs=in_vmem(),
        compiler_params=pltpu.CompilerParams(vmem_limit_bytes=KERNEL_VMEM),
        name="scale",
    )(rows, gain)


def half_columns(width):
    half = lax.axis_index("dp")
    return [pl.ds(pl.multiple_of(h * width, LANES), width) for h in (half, 1 - half)]


def dot(rows, weights):
    return jnp.dot(rows, weights, preferred_element_type=jnp.float32)


def early_kernel(fanout, offset, *refs):
    own, one, two, own_p, one_p, two_p, gate_ref, up_ref = refs[:8]
    gate_acc, up_acc, facts_ref, near_rows, far_rows, lines_ref = refs[8:]
    chunk, width = near_rows.shape[0] // 4, near_rows.shape[1]
    expert = lax.axis_index("expert")
    first = lax.rem(expert, 2) == 0
    near_at, far_at = half_columns(width)

    lines_ref[...] = jnp.zeros_like(lines_ref)

    def fill(rows_ref, before, pieces):
        for i, piece in enumerate(pieces):
            for at, columns in tiles(chunk, width):
                rows_ref[i * chunk : (i + 1) * chunk, columns] = piece[at, :]
            place = (before + i) * FACTS
            lines_ref[place : place + FACTS, :] = piece[piece.shape[0] - FACTS :, :].astype(jnp.float32)

    @pl.when(first)
    def _():
        fill(near_rows, 0, (own, own_p, two, one_p))
        fill(far_rows, 4, (one, two_p))

    @pl.when(jnp.logical_not(first))
    def _():
        fill(near_rows, 0, (own, own_p, one, two_p))
        fill(far_rows, 4, (two, one_p))

    this = 2 * chunk
    step = min(gate_ref.shape[1], 256)
    for start in range(0, gate_ref.shape[1], step):
        columns = pl.ds(start, step)
        for weights, acc in ((gate_ref, gate_acc), (up_ref, up_acc)):
            near = dot(near_rows[...], weights[near_at, columns])
            acc[:this, columns] = near[:this] + dot(far_rows[...], weights[far_at, columns])
            acc[this:, columns] = near[this:]

    about = lines_ref[...].T[offset : offset + chunk, :]

    def column(fact, pieces):
        return jnp.concatenate(
            [about[:, i * FACTS + fact : i * FACTS + fact + 1] for i in pieces], axis=0
        )

    total, mine = 0.0, 0.0
    for k in range(fanout):
        level = column(fanout + k, range(4))
        total = total + level
        mine = mine + jnp.where(column(k, range(4)) == expert.astype(jnp.float32), level, 0.0)
    squares = column(2 * fanout, range(4)) + column(2 * fanout + 1, range(4))
    far = column(2 * fanout, (4, 5)) + column(2 * fanout + 1, (4, 5))
    lane = lax.broadcasted_iota(jnp.int32, (this, LANES), 1)
    share = mine / total
    facts_ref[:this, :] = jnp.where(lane == 0, share[:this], squares[:this] + far)
    facts_ref[this:, :] = jnp.where(lane == 0, share[this:], squares[this:])


def down_product(hidden_ref, down_ref, far_side, width, store):
    hidden = hidden_ref[...]
    chunk = hidden.shape[0] // 4
    half = lax.axis_index("dp")
    wide = 256 if width % 256 == 0 else width
    for start in range(0, width, wide):
        base = (1 - half if far_side else half) * width + start
        value = dot(hidden, down_ref[:, pl.ds(pl.multiple_of(base, LANES), wide)])
        store(pl.ds(start, wide), *[value[i * chunk : (i + 1) * chunk] for i in range(4)])


def late_kernel(fanout, offset, *refs):
    corner, corner_p, gate_acc, up_acc, facts_ref, gate_ref, up_ref, down_ref = refs[:8]
    hidden_ref, corner_out, corner_p_out, far_out, far_p_out, corner_rows = refs[8:]
    chunk, width = corner_out.shape
    this = 2 * chunk
    far_at = half_columns(width)[1]
    lines = []
    for i, piece in enumerate((corner, corner_p)):
        for at, columns in tiles(chunk, width):
            corner_rows[i * chunk : (i + 1) * chunk, columns] = piece[at, :]
        lines.append(piece[piece.shape[0] - FACTS :, :].astype(jnp.float32))
    lines.append(jnp.zeros((LANES - 2 * FACTS, LANES), jnp.float32))
    about = jnp.concatenate(lines, axis=0).T[offset : offset + chunk, :]
    high, low = 2 * fanout, 2 * fanout + 1
    far = [
        about[:, i + high : i + high + 1] + about[:, i + low : i + low + 1] for i in (0, FACTS)
    ]
    share, squares = facts_ref[:, :1], facts_ref[:, 1:2]
    squares = jnp.concatenate([squares[:this], squares[this:] + jnp.concatenate(far, axis=0)], axis=0)
    inverse = lax.rsqrt(squares / gate_ref.shape[0] + epsilon)
    step = min(gate_ref.shape[1], 256)
    for start in range(0, gate_ref.shape[1], step):
        columns = pl.ds(start, step)
        gate_corner = dot(corner_rows[...], gate_ref[far_at, columns])
        up_corner = dot(corner_rows[...], up_ref[far_at, columns])
        for at, gate_more, up_more in ((slice(0, this), 0.0, 0.0), (slice(this, None), gate_corner, up_corner)):
            gate = inverse[at] * (gate_acc[at, columns] + gate_more)
            up = inverse[at] * (up_acc[at, columns] + up_more)
            value = jnp.where(share[at] > 0.0, jax.nn.silu(gate) * up * share[at], 0.0)
            hidden_ref[at, columns] = value.astype(jnp.bfloat16)

    def store(at, here, here_p, other, other_p):
        corner_out[:, at] = other.astype(jnp.bfloat16)
        corner_p_out[:, at] = other_p.astype(jnp.bfloat16)
        far_out[:, at] = here.astype(jnp.bfloat16)
        far_p_out[:, at] = here_p.astype(jnp.bfloat16)

    down_product(hidden_ref, down_ref, True, width, store)


def last_kernel(kept, hidden_ref, far, far_p, down_ref, stay, along, along_p, stay_p):
    role = lax.rem(lax.axis_index("expert"), 2)
    chunk = stay.shape[0]
    along[role, :, :] = far[...]
    along_p[1 - role, :, :] = far_p[...]

    def store(at, here, here_p, other, other_p):
        for k in range(here.shape[1] // LANES):
            columns = pl.ds(at.start + k * LANES, LANES)
            rows = pl.ds((at.start // LANES + k) * chunk, chunk)
            stay[:, columns] = kept[rows, :].astype(jnp.float32) + here[:, k * LANES : (k + 1) * LANES]
        stay_p[:, at] = here_p.astype(jnp.bfloat16)
        along[1 - role, :, at] = other.astype(jnp.bfloat16)
        along_p[role, :, at] = other_p.astype(jnp.bfloat16)

    down_product(hidden_ref, down_ref, False, stay.shape[1], store)


def join_kernel(moved, stay, stay_p, second, third, out_hbm, sum_ref, sems):
    chunk = moved.shape[0]
    first = pltpu.make_async_copy(moved, out_hbm.at[pl.ds(0, chunk), :], sems.at[0])
    first.start()
    total = stay[...] + stay_p[...].astype(jnp.float32)
    total = total + second[...].astype(jnp.float32) + third[...].astype(jnp.float32)
    sum_ref[...] = total.astype(jnp.bfloat16)
    rest = pltpu.make_async_copy(sum_ref, out_hbm.at[pl.ds(chunk, sum_ref.shape[0]), :], sems.at[1])
    rest.start()
    first.wait()
    rest.wait()


def join(moved, stay, *pieces):
    rows, width = stay.shape
    return pl.pallas_call(
        join_kernel,
        out_shape=jax.ShapeDtypeStruct((moved.shape[0] + rows, width), jnp.bfloat16),
        in_specs=[in_vmem()] * 5,
        out_specs=in_hbm(),
        scratch_shapes=[pltpu.VMEM((rows, width), jnp.bfloat16), pltpu.SemaphoreType.DMA((2,))],
        compiler_params=pltpu.CompilerParams(vmem_limit_bytes=KERNEL_VMEM),
        name="join",
    )(moved, stay, *pieces)


def early_block(mine, theirs, w_gate, w_up, fanout, offset):
    width = w_gate.shape[0] // lax.axis_size("dp")
    chunk = (mine[0].shape[0] - FACTS) * LANES // width
    rows, units = 4 * chunk, w_gate.shape[1]
    f32 = functools.partial(jax.ShapeDtypeStruct, dtype=jnp.float32)
    return pl.pallas_call(
        functools.partial(early_kernel, fanout, offset),
        out_shape=[f32((rows, units)), f32((rows, units)), f32((rows, LANES))],
        in_specs=[in_vmem()] * 8,
        out_specs=[in_vmem()] * 3,
        scratch_shapes=[
            pltpu.VMEM((rows, width), jnp.bfloat16),
            pltpu.VMEM((rows // 2, width), jnp.bfloat16),
            pltpu.VMEM((LANES, LANES), jnp.float32),
        ],
        compiler_params=pltpu.CompilerParams(vmem_limit_bytes=KERNEL_VMEM),
        cost_estimate=pl.CostEstimate(
            flops=3 * rows * w_gate.size, bytes_accessed=4 * w_gate.size, transcendentals=0
        ),
        name="early",
    )(*mine[:3], *theirs[:3], w_gate, w_up)


def late_block(corner, corner_p, partial, w_gate, w_up, w_down, fanout, offset):
    width = w_gate.shape[0] // lax.axis_size("dp")
    chunk = (corner.shape[0] - FACTS) * LANES // width
    rows, units = 4 * chunk, w_gate.shape[1]
    piece = functools.partial(jax.ShapeDtypeStruct, dtype=jnp.bfloat16)
    return pl.pallas_call(
        functools.partial(late_kernel, fanout, offset),
        out_shape=[piece((rows, units))] + [piece((chunk, width))] * 4,
        in_specs=[in_vmem()] * 8,
        out_specs=[in_vmem()] * 5,
        scratch_shapes=[pltpu.VMEM((rows // 2, width), jnp.bfloat16)],
        compiler_params=pltpu.CompilerParams(vmem_limit_bytes=KERNEL_VMEM),
        cost_estimate=pl.CostEstimate(
            flops=2 * rows * w_gate.size, bytes_accessed=5 * w_gate.size, transcendentals=0
        ),
        name="late",
    )(corner, corner_p, *partial, w_gate, w_up, w_down)


def last_block(kept, hidden, far, far_p, w_down):
    chunk, width = far.shape
    piece = functools.partial(jax.ShapeDtypeStruct, dtype=jnp.bfloat16)
    two = piece((2, chunk, width))
    return pl.pallas_call(
        last_kernel,
        out_shape=[jax.ShapeDtypeStruct((chunk, width), jnp.float32), two, two, piece((chunk, width))],
        in_specs=[in_vmem()] * 5,
        out_specs=[in_vmem()] * 4,
        compiler_params=pltpu.CompilerParams(vmem_limit_bytes=KERNEL_VMEM),
        cost_estimate=pl.CostEstimate(
            flops=4 * chunk * w_down.size, bytes_accessed=w_down.size, transcendentals=0
        ),
        name="last",
    )(kept, hidden, far, far_p, w_down)


def plus(*values):
    total = values[0].astype(jnp.float32)
    for value in values[1:]:
        total = total + value.astype(jnp.float32)
    return total.astype(jnp.bfloat16)


def dense_body(tokens, expert_ids, gate_levels, gain, w_gate, w_up, w_down):
    fanout = expert_ids.shape[2]
    here, kept, away, gain_rows = pack(
        tokens[0], gain, expert_ids[0].T, gate_levels[0].T, tokens.shape[1] // 2
    )
    gain_rows = spread(gain_rows)
    for part in range(2):
        offset = part * (tokens.shape[1] // 2)
        if part == 1:
            kept = from_behind(away, "pipe", 1)
            own = scale(kept, gain_rows)
        else:
            own = here
        one = across(own, True)
        two = across(own, False)
        corner = across(one, False)
        mine = [own, one, two, corner]
        theirs = [to_partner(v) for v in mine]
        weights = (w_gate[0], w_up[0], w_down[0])
        partial = early_block(mine, theirs, *weights[:2], fanout, offset)
        hidden, corner, corner_p, far, far_p = late_block(
            mine[3], theirs[3], partial, *weights, fanout, offset
        )
        corner_p = to_partner(corner_p)
        stay, along, along_p, stay_p = last_block(kept, hidden, far, far_p, weights[2])
        corner = plus(corner, corner_p)
        along_p = to_partner(along_p)
        second = plus(along[0], along_p[0])
        got_corner = across(corner, True)
        got_second = across(second, True)
        third = plus(along[1], along_p[1], got_corner)
        got_third = across(third, False)
        stay_p = to_partner(stay_p)
        if part == 0:
            out = plus(stay, stay_p, got_second, got_third)
            moved = from_behind(out, "pipe", 1)
        else:
            out = join(moved, stay, stay_p, got_second, got_third)
    return out[None]


def solution(mesh):
    specs = dict(
        mesh=mesh,
        in_specs=(
            P("pipe", "expert", "dp"),
            P("pipe", "expert", None),
            P("pipe", "expert", None),
            P("dp"),
            P("expert", None, "dp"),
            P("expert", None, "dp"),
            P("expert", "dp", None),
        ),
        out_specs=P("pipe", "expert", "dp"),
        check_vma=False,
    )
    if mesh.shape["expert"] == 4 and mesh.shape["dp"] == 2:
        return jax.shard_map(dense_body, **specs)
    return jax.shard_map(routed_body, **specs)
```
